256 devices in a mesh: ctx: 128 (over z, y, x), head: 2 (over core).
Axes of the slice: x: 4, y: 4, z: 8, core: 2. Of those that a mesh axis runs over, the one named last changes fastest.
Arguments:
- queries: bfloat16 [32768, 4096], P('ctx', 'head'), may hold values from -6.5 to 6.5
- keyval: bfloat16 [2, 32768, 1024], P(None, 'ctx', 'head'), may hold values from -6 to 6
- out_gain: float32 [4096], P('head'), may hold values from 0.1 to 1.9
Outputs:
- attended: bfloat16 [32768, 4096], P('ctx', 'head')
The draws below stay inside these ranges and needn't reach their ends.
All inputs are finite; a program needn't handle non-finite values.
Results may differ from the reference program's by a relative error of at most 0.0049.
Values may be sent and summed in bfloat16 or wider, within the bound.
No kernel may reach another device: no remote copies, remote signals or barrier semaphores. Data moves between devices by JAX's collectives and lax.ppermute only.
A program may use at most 64 MiB of HBM per device.

```python
import jax
import jax.numpy as jnp
from jax import lax

HEADS = 32
KV_HEADS = 8
HD = 128
BLK = 128
TOKENS = 32768


def draw_queries(key, part):
    group_size = HEADS // KV_HEADS
    result = jnp.clip(jax.random.normal(jax.random.fold_in(key, 21), (TOKENS, KV_HEADS, group_size, HD), jnp.float32), -6.0, 6.0)
    return result.reshape(TOKENS, HEADS * HD).astype(jnp.bfloat16)


def draw_keyval(key, part):
    value_part = jnp.clip(jax.random.normal(jax.random.fold_in(key, 32), (TOKENS, KV_HEADS * HD), jnp.float32), -6.0, 6.0)
    key_part = jnp.clip(jax.random.normal(jax.random.fold_in(key, 31), (TOKENS, KV_HEADS, HD), jnp.float32), -6.0, 6.0)
    return jnp.stack([key_part.reshape(TOKENS, KV_HEADS * HD), value_part]).astype(jnp.bfloat16)


def setup_inputs(seed: int = 0) -> dict:
    streams_of = jax.random.split(jax.random.key(seed), 4)
    return {
        "queries": draw_queries(jax.random.fold_in(streams_of[3], 71), 0),
        "keyval": draw_keyval(jax.random.fold_in(streams_of[3], 71), 0),
        "out_gain": jnp.clip(1.0 + 0.18 * jax.random.normal(streams_of[2], (HEADS * HD,), jnp.float32), 0.1, 1.9),
    }


def reference(queries, keyval, out_gain):
    tok_total = queries.shape[0]
    nblocks = tok_total // BLK
    group_size = HEADS // KV_HEADS
    gap_list = jnp.array([0] + [2 ** power_exp for power_exp in range(nblocks.bit_length() - 1)], jnp.int32)
    q_blocks = queries.reshape(nblocks, BLK, KV_HEADS, group_size, HD)
    kv_blocks = keyval.reshape(2, nblocks, BLK, KV_HEADS, HD)
    lower_tri = jnp.arange(BLK)[:, None] >= jnp.arange(BLK)[None, :]
    own_slot = jnp.arange(gap_list.shape[0]) == 0
    score_scale = HD ** (-0.5)

    def one_block(block_id):
        sources = block_id - gap_list
        valid_slot = sources >= 0
        picks = jnp.maximum(sources, 0).astype(jnp.int32)
        key_rows = kv_blocks[0][picks]
        value_rows = kv_blocks[1][picks]
        query_rows = lax.dynamic_index_in_dim(q_blocks, block_id, 0, keepdims=False)
        scores = jnp.einsum('qhgd,skhd->hgqsk', query_rows.astype(jnp.float32), key_rows.astype(jnp.float32)) * score_scale
        allowed = valid_slot[None, :, None] & (own_slot[None, :, None] | lower_tri[:, None, :])
        scores = jnp.where(allowed[None, None], scores, -jnp.inf)
        row_max = lax.optimization_barrier(jnp.max(scores, axis=(3, 4), keepdims=True))
        weights = jnp.exp(scores - row_max)
        row_sum = lax.optimization_barrier(jnp.sum(weights, axis=(3, 4), keepdims=True))
        probabilities = (weights / row_sum).astype(jnp.bfloat16)
        return jnp.einsum('hgqsk,skhd->qhgd', probabilities.astype(jnp.float32), value_rows.astype(jnp.float32))
    outputs = lax.map(one_block, jnp.arange(nblocks, dtype=jnp.int32))
    combined = outputs.reshape(tok_total, HEADS * HD)
    squares = lax.optimization_barrier(jnp.sum(combined * combined, axis=1))
    inverse = lax.rsqrt(squares / (HEADS * HD) + 1e-06)
    return (combined * inverse[:, None] * out_gain[None, :]).astype(jnp.bfloat16)
```

```python
import functools

import jax
import jax.numpy as jnp
from jax import lax
from jax.experimental import pallas as pl
from jax.experimental.pallas import tpu as pltpu
from jax.sharding import PartitionSpec as P

HEADS = 32
HD = 128
BLK = 128
NZ, NY, NX = 8, 4, 4
NEG = -1e30


def ring(dz, dy, dx):
    return [
        (
            (z * NY + y) * NX + x,
            ((z + dz) % NZ * NY + (y + dy) % NY) * NX + (x + dx) % NX,
        )
        for z in range(NZ)
        for y in range(NY)
        for x in range(NX)
    ]


def send(value, dz, dy, dx):
    return lax.ppermute(value, "ctx", ring(dz, dy, dx))


def attend_kernel(bias_ref, q_ref, own_ref, *refs):
    panels = refs[:14]
    comb_ref, sq_ref = refs[14:]
    keys = [own_ref.at[0]] + [panels[2 * i] for i in range(7)]
    vals = [own_ref.at[1]] + [panels[2 * i + 1] for i in range(7)]
    group = q_ref.shape[1] // HD
    factor = HD ** (-0.5) * 1.4426950408889634
    row = lax.broadcasted_iota(jnp.int32, (BLK, BLK), 0)
    col = lax.broadcasted_iota(jnp.int32, (BLK, BLK), 1)
    tri = jnp.where(row >= col, 0.0, NEG).astype(jnp.float32)
    ones = jnp.ones((BLK, HD), jnp.bfloat16)
    for b in range(2):
        rows = slice(b * BLK, (b + 1) * BLK)
        qs = jnp.concatenate([q_ref[rows, h * HD : (h + 1) * HD] for h in range(group)], axis=0)
        slots = [(0, b), (0, 0) if b else (1, 1)] + [(i, b) for i in range(1, 8)]
        kcat = jnp.concatenate([keys[i][j * BLK : (j + 1) * BLK, :] for i, j in slots], axis=0)
        vcat = jnp.concatenate(
            [jnp.concatenate([vals[i][j * BLK : (j + 1) * BLK, :], ones], axis=1) for i, j in slots], axis=0
        )
        raw = lax.dot_general(qs, kcat, (((1,), (1,)), ((), ())), preferred_element_type=jnp.float32)
        parts = []
        for n, (i, j) in enumerate(slots):
            part = raw[:, n * BLK : (n + 1) * BLK]
            if n:
                mask = tri + bias_ref[i] if i else tri
                part = part + jnp.concatenate([mask] * group, axis=0)
            parts.append(part)
        top = functools.reduce(jnp.maximum, parts)
        top = jnp.max(top, axis=1, keepdims=True)
        probs = jnp.concatenate([jnp.exp2((part - top) * factor).astype(jnp.bfloat16) for part in parts], axis=1)
        both = lax.dot_general(probs, vcat, (((1,), (0,)), ((), ())), preferred_element_type=jnp.float32)
        comb = both[:, :HD] / both[:, HD:]
        total = jnp.zeros((BLK, HD), jnp.float32)
        for h in range(group):
            piece = comb[h * BLK : (h + 1) * BLK]
            comb_ref[rows, h * HD : (h + 1) * HD] = piece
            total = total + piece * piece

        @pl.when(pl.program_id(0) == 0)
        def _():
            sq_ref[rows, :] = total

        @pl.when(pl.program_id(0) > 0)
        def _():
            sq_ref[rows, :] = sq_ref[rows, :] + total


def norm_kernel(comb_ref, mine_ref, other_ref, gain_ref, out_ref):
    total = jnp.sum(mine_ref[...] + other_ref[...], axis=1, keepdims=True)
    inverse = lax.rsqrt(total / (HEADS * HD) + 1e-06)
    out_ref[...] = (comb_ref[...] * inverse * gain_ref[...]).astype(jnp.bfloat16)


def local(queries, keyval, out_gain):
    tok_rows, width = queries.shape
    kv_local = keyval.shape[2] // HD
    place = lax.axis_index("ctx")
    y = place // NX % NY
    x = place % NX
    own = [keyval[0], keyval[1]]
    r16 = [send(c, 1, 0, 0) for c in own]
    mid = send(own[1], -2, 0, 0)
    r64k = send(own[0], 4, 0, 0)
    r4 = [send(jnp.where(y == NY - 1, a, c), 0, 1, 0) for a, c in zip(r16, own)]
    r64 = [r64k, send(mid, -2, 0, 0)]
    r32 = [send(a, 1, 0, 0) for a in r16]
    r8 = [send(jnp.where(y >= 2, a, c), 0, 2, 0) for a, c in zip(r16, own)]
    r1 = [send(jnp.where(x == NX - 1, a, c), 0, 0, 1) for a, c in zip(r4, own)]
    far = [jnp.where(x >= 2, a, c) for a, c in zip(r4, own)]
    r2 = [send(far[0], 0, 0, 2), send(send(far[1], 0, 0, -1), 0, 0, -1)]
    panels = [r1, r2, r4, r8, r16, r32, r64]
    reach = jnp.array([0] + [2**i for i in range(7)], jnp.int32)
    bias = jnp.where(place >= reach, 0.0, NEG).astype(jnp.float32)

    step = width // kv_local
    half_spec = pl.BlockSpec((tok_rows, HD), lambda g: (0, g))
    comb, squares = pl.pallas_call(
        attend_kernel,
        grid=(kv_local,),
        in_specs=[
            pl.BlockSpec(memory_space=pltpu.SMEM),
            pl.BlockSpec((tok_rows, step), lambda g: (0, g)),
            pl.BlockSpec((2, tok_rows, HD), lambda g: (0, 0, g)),
        ]
        + [half_spec] * 14,
        out_specs=[
            pl.BlockSpec((tok_rows, step), lambda g: (0, g)),
            pl.BlockSpec((tok_rows, HD), lambda g: (0, 0)),
        ],
        out_shape=[
            jax.ShapeDtypeStruct((tok_rows, width), jnp.float32),
            jax.ShapeDtypeStruct((tok_rows, HD), jnp.float32),
        ],
        name="attend",
    )(bias, queries, keyval, *[half for panel in panels for half in panel])
    other = lax.ppermute(squares, "head", [(0, 1), (1, 0)])
    return pl.pallas_call(
        norm_kernel,
        grid=(2,),
        in_specs=[
            pl.BlockSpec((tok_rows // 2, width), lambda i: (i, 0)),
            pl.BlockSpec((tok_rows // 2, HD), lambda i: (i, 0)),
            pl.BlockSpec((tok_rows // 2, HD), lambda i: (i, 0)),
            pl.BlockSpec((1, width), lambda i: (0, 0)),
        ],
        out_specs=pl.BlockSpec((tok_rows // 2, width), lambda i: (i, 0)),
        out_shape=jax.ShapeDtypeStruct((tok_rows, width), jnp.bfloat16),
        name="norm",
    )(comb, squares, other, out_gain[None, :])


def solution(mesh):
    in_specs = (P("ctx", "head"), P(None, "ctx", "head"), P("head"))
    out_specs = P("ctx", "head")
    return jax.shard_map(local, mesh=mesh, in_specs=in_specs, out_specs=out_specs, check_vma=False)
```

```python
import functools

import jax
import jax.numpy as jnp
from jax import lax
from jax.experimental import pallas as pl
from jax.experimental.pallas import tpu as pltpu
from jax.sharding import PartitionSpec as P

HEADS = 32
HD = 128
BLK = 128
NZ, NY, NX = 8, 4, 4
NEG = -1e30
FACTOR = HD ** (-0.5) * 1.4426950408889634
VMEM = pl.BlockSpec(memory_space=pltpu.VMEM)
PARAMS = pltpu.CompilerParams(vmem_limit_bytes=16 << 20)


def on_chip(value):
    return pltpu.with_memory_space_constraint(value, pltpu.VMEM)


def ring(dz, dy, dx):
    return [
        (
            (z * NY + y) * NX + x,
            ((z + dz) % NZ * NY + (y + dy) % NY) * NX + (x + dx) % NX,
        )
        for z in range(NZ)
        for y in range(NY)
        for x in range(NX)
    ]


def send(value, dz, dy, dx):
    return lax.ppermute(value, "ctx", ring(dz, dy, dx))


def lanes(index):
    return pl.ds(index * HD if isinstance(index, int) else pl.multiple_of(index * HD, HD), HD)


def triangle():
    row = lax.broadcasted_iota(jnp.int32, (BLK, BLK), 0)
    col = lax.broadcasted_iota(jnp.int32, (BLK, BLK), 1)
    return jnp.where(row >= col, 0.0, NEG).astype(jnp.float32)


def gather_slots(panels, slots, g):
    ones = jnp.ones((BLK, HD), jnp.bfloat16)
    cut = lambda ref, j: ref[j * BLK : (j + 1) * BLK, lanes(g)]
    keys = jnp.concatenate([cut(panels[i][0], j) for i, j in slots], axis=0)
    vals = [jnp.concatenate([cut(panels[i][1], j), ones], axis=1) for i, j in slots]
    return keys, jnp.concatenate(vals, axis=0)


def score_parts(query, keys, masks):
    raw = lax.dot_general(query, keys, (((1,), (1,)), ((), ())), preferred_element_type=jnp.float32)
    parts = [raw[:, n * BLK : (n + 1) * BLK] for n in range(len(masks))]
    parts = [part if mask is None else part + mask for part, mask in zip(parts, masks)]
    top = jnp.max(functools.reduce(jnp.maximum, parts), axis=1, keepdims=True)
    return parts, top


def weigh(parts, top, vals):
    probs = [jnp.exp2((part - top) * FACTOR).astype(jnp.bfloat16) for part in parts]
    probs = jnp.concatenate(probs, axis=1)
    return lax.dot_general(probs, vals, (((1,), (0,)), ((), ())), preferred_element_type=jnp.float32)


def masks_of(slots, b):
    tri = triangle()
    place = lax.axis_index("ctx")
    masks = []
    for i, j in slots:
        if i == 0:
            masks.append(None if j == b else tri)
        else:
            masks.append(tri + jnp.where(place >= 2 ** (i - 1), 0.0, NEG))
    return masks


def split_kernel(kv_ref, k_ref, v_ref, sems):
    copies = [pltpu.make_async_copy(kv_ref.at[n], ref, sems.at[n]) for n, ref in enumerate((k_ref, v_ref))]
    for copy in copies:
        copy.start()
    for copy in copies:
        copy.wait()


def choose(moved, come_ref, own_ref, out_ref):
    @pl.when(moved)
    def _():
        out_ref[...] = come_ref[...]

    @pl.when(jnp.logical_not(moved))
    def _():
        out_ref[...] = own_ref[...]


def reaches(test):
    shift, least = test
    return ((lax.axis_index("ctx") >> shift) & 3) >= least


def pick_kernel(come_ref, own_ref, *outs, tests):
    for out_ref, test in zip(outs, tests):
        choose(reaches(test), come_ref, own_ref, out_ref)


def pick_both_kernel(come_k_ref, own_k_ref, come_v_ref, own_v_ref, near_ref, far_ref):
    choose(reaches(ROWS), come_v_ref, own_v_ref, near_ref)
    far = reaches(HALF_ROWS)
    choose(far, come_k_ref, own_k_ref, far_ref.at[0])
    choose(far, come_v_ref, own_v_ref, far_ref.at[1])


def stage_kernel(source_ref, *refs, ids, group, first, last):
    panels = {}
    q_ref = refs[-2] if first else source_ref
    for i in ids:
        if i == WHOLE:
            panels[i], refs = (refs[0].at[0], refs[0].at[1]), refs[1:]
        else:
            panels[i], refs = refs[:2], refs[2:]
    if not first:
        old_acc_ref, old_top_ref = refs[:2]
        refs = refs[2:]
    if last:
        comb_ref, sq_ref, total_ref = refs
        total_ref[...] = jnp.zeros_like(total_ref)
    else:
        acc_ref, top_ref = refs[:2]
    if first:
        width = group * HD
        loads = [
            pltpu.make_async_copy(source_ref.at[:, part], q_ref.at[:, part], refs[-1].at[n])
            for n, part in enumerate(pl.ds(n * width, width) for n in range(q_ref.shape[1] // width))
        ]
        for load in loads:
            load.start()

    def body(g, carry):
        for b in range(2):
            rows = slice(b * BLK, (b + 1) * BLK)
            slots = [(i, b) for i in ids]
            if b and 0 in ids:
                slots = slots + [(0, 0)]
            if not b and 1 in ids:
                slots = slots + [(1, 1)]
            masks = masks_of(slots, b)
            keys, vals = gather_slots(panels, slots, g)
            if last:
                total = total_ref[rows, :]
            for h in range(group):
                head = g * group + h
                unit = head * 2 + b
                parts, top = score_parts(q_ref[rows, lanes(head)], keys, masks)
                if first:
                    acc = weigh(parts, top, vals)
                else:
                    old = old_top_ref[unit]
                    top = jnp.maximum(old, top)
                    scale = jnp.exp2((old - top) * FACTOR)
                    both = weigh(parts, top, vals)
                    acc = old_acc_ref[unit] * jnp.concatenate([scale, scale], axis=1) + both
                if last:
                    comb = acc[:, :HD] / acc[:, HD:]
                    comb_ref[rows, lanes(head)] = comb
                    total = total + comb * comb
                else:
                    acc_ref[unit] = acc
                    top_ref[unit] = jnp.broadcast_to(top, (BLK, HD))
            if last:
                total_ref[rows, :] = total
        return carry

    if first:
        for g, load in enumerate(loads):
            load.wait()
            body(g, 0)
    else:
        lax.fori_loop(0, q_ref.shape[1] // HD // group, body, 0, unroll=UNROLL)
    if last:
        sq_ref[...] = lax.dot_general(
            jnp.ones((8, HD), jnp.float32),
            total_ref[...],
            (((1,), (1,)), ((), ())),
            preferred_element_type=jnp.float32,
            precision=lax.Precision.HIGHEST,
        )


def norm_kernel(comb_ref, mine_ref, other_ref, gain_ref, out_ref, buf, sems):
    rows, width = comb_ref.shape
    square_sum = mine_ref[...] + other_ref[...]
    inverse = lax.rsqrt(square_sum / (HEADS * HD) + 1e-06)[:1]
    inverse = jnp.transpose(jnp.broadcast_to(inverse, (HD, rows)))
    inverse = jnp.concatenate([inverse] * (width // HD), axis=1)
    step = rows // 4
    copies = []
    for n in range(4):
        part = slice(n * step, (n + 1) * step)
        buf[part, :] = (comb_ref[part, :] * inverse[part] * gain_ref[...]).astype(jnp.bfloat16)
        copies.append(pltpu.make_async_copy(buf.at[part], out_ref.at[part], sems.at[n]))
        copies[-1].start()
    for copy in copies:
        copy.wait()


def split(keyval):
    half = pltpu.VMEM(keyval.shape[1:], keyval.dtype)
    pair = pl.pallas_call(
        split_kernel,
        in_specs=[pl.BlockSpec(memory_space=pltpu.HBM)],
        out_specs=[VMEM, VMEM],
        out_shape=[half, half],
        scratch_shapes=[pltpu.SemaphoreType.DMA((2,))],
        compiler_params=PARAMS,
        name="split",
    )(pltpu.with_memory_space_constraint(keyval, pltpu.HBM))
    return [on_chip(half) for half in pair]


def pick(come, own, *tests):
    outs = pl.pallas_call(
        functools.partial(pick_kernel, tests=tests),
        in_specs=[VMEM, VMEM],
        out_specs=[VMEM] * len(tests),
        out_shape=[pltpu.VMEM(own.shape, own.dtype)] * len(tests),
        compiler_params=PARAMS,
        name="pick",
    )(on_chip(come), own)
    return [on_chip(out) for out in outs]


def pick_both(come_k, own_k, come_v, own_v):
    outs = pl.pallas_call(
        pick_both_kernel,
        in_specs=[VMEM] * 4,
        out_specs=[VMEM] * 2,
        out_shape=[pltpu.VMEM(own_v.shape, own_v.dtype), pltpu.VMEM((2, *own_v.shape), own_v.dtype)],
        compiler_params=PARAMS,
        name="pick_both",
    )(on_chip(come_k), own_k, on_chip(come_v), own_v)
    return [on_chip(out) for out in outs]


def attend(queries, panels, ids, group, state, last):
    rows, width = queries.shape
    count = width // HD * (rows // BLK)
    if last:
        shapes = [pltpu.VMEM((rows, width), jnp.float32), pltpu.VMEM((8, rows), jnp.float32)]
    else:
        shapes = [pltpu.VMEM((count, BLK, 2 * HD), jnp.float32), pltpu.VMEM((count, BLK, HD), jnp.float32)]
    scratch = [pltpu.VMEM((rows, HD), jnp.float32)] if last else []
    first = not state
    halves = [half for i in ids for half in panels[i]]
    source = VMEM
    if first:
        shapes.append(pltpu.VMEM((rows, width), jnp.bfloat16))
        scratch.append(pltpu.SemaphoreType.DMA((width // HD // group,)))
        source = pl.BlockSpec(memory_space=pltpu.HBM)
    outs = pl.pallas_call(
        functools.partial(stage_kernel, ids=ids, group=group, first=first, last=last),
        in_specs=[source] + [VMEM] * (len(halves) + len(state)),
        out_specs=[VMEM] * len(shapes),
        out_shape=shapes,
        scratch_shapes=scratch,
        compiler_params=PARAMS,
        name="stage",
    )(queries, *halves, *state)
    return [on_chip(out) for out in outs]


UNROLL = 2
WHOLE = 4
STAGES = ((0,), (5, 3), (6, 1), (4, 2, 7))
ROWS, HALF_ROWS, COLS, HALF_COLS = (2, 3), (2, 2), (0, 3), (0, 2)


def local(queries, keyval, out_gain):
    tok_rows, width = queries.shape
    group = width // keyval.shape[2]
    own = split(keyval)
    r16 = [send(own[0], 1, 0, 0), send(own[1], 1, 0, 0)]
    mid = send(own[1], -1, 0, 0)
    r32 = [send(r16[0], 1, 0, 0), send(r16[1], 1, 0, 0)]
    r64 = [send(r32[0], 2, 0, 0), send(mid, -3, 0, 0)]
    (near,) = pick(r16[0], own[0], ROWS)
    r4k = send(near, 0, 1, 0)
    near, far = pick_both(r16[0], own[0], r16[1], own[1])
    r4 = [r4k, send(near, 0, 1, 0)]
    r8 = [send(far, 0, 2, 0)]
    near, far = pick(r4[0], own[0], COLS, HALF_COLS)
    r1k = send(near, 0, 0, 1)
    r2k = send(send(far, 0, 0, -1), 0, 0, -1)
    near, far = pick(r4[1], own[1], COLS, HALF_COLS)
    r1 = [r1k, send(near, 0, 0, 1)]
    r2 = [r2k, send(far, 0, 0, 2)]
    panels = [[on_chip(half) for half in panel] for panel in (own, r1, r2, r4, r8, r16, r32, r64)]
    query = pltpu.with_memory_space_constraint(queries, pltpu.HBM)
    state = []
    for n, ids in enumerate(STAGES):
        state = attend(query, panels, ids, group, state, n == len(STAGES) - 1)
        if n == 0:
            *state, query = state
    comb, squares = state
    other = on_chip(lax.ppermute(squares, "head", [(0, 1), (1, 0)]))
    return pl.pallas_call(
        norm_kernel,
        in_specs=[VMEM] * 4,
        out_specs=pl.BlockSpec(memory_space=pl.ANY),
        out_shape=jax.ShapeDtypeStruct((tok_rows, width), jnp.bfloat16),
        scratch_shapes=[pltpu.VMEM((tok_rows, width), jnp.bfloat16), pltpu.SemaphoreType.DMA((4,))],
        compiler_params=PARAMS,
        name="norm",
    )(comb, squares, other, on_chip(out_gain[None, :]))


def solution(mesh):
    in_specs = (P("ctx", "head"), P(None, "ctx", "head"), P("head"))
    out_specs = P("ctx", "head")
    return jax.shard_map(local, mesh=mesh, in_specs=in_specs, out_specs=out_specs, check_vma=False)
```

```python
import functools

import jax
import jax.numpy as jnp
from jax import lax
from jax.experimental import pallas as pl
from jax.experimental.pallas import tpu as pltpu
from jax.sharding import PartitionSpec as P

HEADS = 32
HD = 128
BLK = 128
NZ, NY, NX = 8, 4, 4
NEG = -1e30
FACTOR = HD ** (-0.5) * 1.4426950408889634
VMEM = pl.BlockSpec(memory_space=pltpu.VMEM)
PARAMS = pltpu.CompilerParams(vmem_limit_bytes=16 << 20)


def on_chip(value):
    return pltpu.with_memory_space_constraint(value, pltpu.VMEM)


def ring(dz, dy, dx):
    return [
        (
            (z * NY + y) * NX + x,
            ((z + dz) % NZ * NY + (y + dy) % NY) * NX + (x + dx) % NX,
        )
        for z in range(NZ)
        for y in range(NY)
        for x in range(NX)
    ]


def send(value, dz, dy, dx):
    return lax.ppermute(value, "ctx", ring(dz, dy, dx))


def lanes(index):
    return pl.ds(index * HD if isinstance(index, int) else pl.multiple_of(index * HD, HD), HD)


def triangle():
    row = lax.broadcasted_iota(jnp.int32, (BLK, BLK), 0)
    col = lax.broadcasted_iota(jnp.int32, (BLK, BLK), 1)
    return jnp.where(row >= col, 0.0, NEG).astype(jnp.float32)


def gather_slots(panels, slots, g):
    ones = jnp.ones((BLK, HD), jnp.bfloat16)
    cut = lambda ref, j: ref[j * BLK : (j + 1) * BLK, lanes(g)]
    keys = jnp.concatenate([cut(panels[i][0], j) for i, j in slots], axis=0)
    vals = [jnp.concatenate([cut(panels[i][1], j), ones], axis=1) for i, j in slots]
    return keys, jnp.concatenate(vals, axis=0)


def score_parts(query, keys, masks):
    raw = lax.dot_general(query, keys, (((1,), (1,)), ((), ())), preferred_element_type=jnp.float32)
    parts = [raw[:, n * BLK : (n + 1) * BLK] for n in range(len(masks))]
    parts = [part if mask is None else part + mask for part, mask in zip(parts, masks)]
    top = jnp.max(functools.reduce(jnp.maximum, parts), axis=1, keepdims=True)
    return parts, top


def weigh(parts, top, vals):
    probs = [jnp.exp2((part - top) * FACTOR).astype(jnp.bfloat16) for part in parts]
    probs = jnp.concatenate(probs, axis=1)
    return lax.dot_general(probs, vals, (((1,), (0,)), ((), ())), preferred_element_type=jnp.float32)


def masks_of(slots, b):
    tri = triangle()
    place = lax.axis_index("ctx")
    masks = []
    for i, j in slots:
        if i == 0:
            masks.append(None if j == b else tri)
        else:
            masks.append(tri + jnp.where(place >= 2 ** ((i - 1) % 7), 0.0, NEG))
    return masks


def split_kernel(kv_ref, k_ref, v_ref, sems):
    copies = [pltpu.make_async_copy(kv_ref.at[n], ref, sems.at[n]) for n, ref in enumerate((k_ref, v_ref))]
    for copy in copies:
        copy.start()
    for copy in copies:
        copy.wait()


def choose(moved, come_ref, own_ref, out_ref):
    @pl.when(moved)
    def _():
        out_ref[...] = come_ref[...]

    @pl.when(jnp.logical_not(moved))
    def _():
        out_ref[...] = own_ref[...]


def reaches(test):
    shift, least = test
    return ((lax.axis_index("ctx") >> shift) & 3) >= least


def pick_kernel(come_ref, own_ref, *outs, tests):
    for out_ref, test in zip(outs, tests):
        choose(reaches(test), come_ref, own_ref, out_ref)


def pick_both_kernel(come_k_ref, own_k_ref, come_v_ref, own_v_ref, near_ref, far_ref):
    choose(reaches(ROWS), come_v_ref, own_v_ref, near_ref)
    far = reaches(HALF_ROWS)
    choose(far, come_k_ref, own_k_ref, far_ref.at[0])
    choose(far, come_v_ref, own_v_ref, far_ref.at[1])


def stage_kernel(source_ref, *refs, ids, group, first, last):
    panels = {}
    q_ref = refs[-2] if first else source_ref
    for i in ids:
        if i == WHOLE:
            panels[i], refs = (refs[0].at[0], refs[0].at[1]), refs[1:]
        else:
            panels[i], refs = refs[:2], refs[2:]
    if not first:
        old_acc_ref, old_top_ref = refs[:2]
        refs = refs[2:]
    if last:
        comb_ref, sq_ref, total_ref = refs
        total_ref[...] = jnp.zeros_like(total_ref)
    else:
        acc_ref, top_ref = refs[:2]
    if first:
        width = group * HD
        loads = [
            pltpu.make_async_copy(source_ref.at[:, part], q_ref.at[:, part], refs[-1].at[n])
            for n, part in enumerate(pl.ds(n * width, width) for n in range(q_ref.shape[1] // width))
        ]
        for load in loads:
            load.start()

    def body(g, carry):
        for b in range(2):
            rows = slice(b * BLK, (b + 1) * BLK)
            slots = [(i, b) for i in ids if i != PREVIOUS]
            if b and 0 in ids:
                slots = slots + [(0, 0)]
            if not b and PREVIOUS in ids:
                slots = slots + [(PREVIOUS, 1)]
            masks = masks_of(slots, b)
            keys, vals = gather_slots(panels, slots, g)
            if last:
                total = total_ref[rows, :]
            for h in range(group):
                head = g * group + h
                unit = head * 2 + b
                parts, top = score_parts(q_ref[rows, lanes(head)], keys, masks)
                if first:
                    acc = weigh(parts, top, vals)
                else:
                    old = old_top_ref[unit]
                    top = jnp.maximum(old, top)
                    scale = jnp.exp2((old - top) * FACTOR)
                    both = weigh(parts, top, vals)
                    acc = old_acc_ref[unit] * jnp.concatenate([scale, scale], axis=1) + both
                if last:
                    comb = acc[:, :HD] / acc[:, HD:]
                    comb_ref[rows, lanes(head)] = comb
                    total = total + comb * comb
                else:
                    acc_ref[unit] = acc
                    top_ref[unit] = jnp.broadcast_to(top, (BLK, HD))
            if last:
                total_ref[rows, :] = total
        return carry

    if first:
        for g, load in enumerate(loads):
            load.wait()
            body(g, 0)
    else:
        lax.fori_loop(0, q_ref.shape[1] // HD // group, body, 0, unroll=UNROLL)
    if last:
        sq_ref[...] = lax.dot_general(
            jnp.ones((8, HD), jnp.float32),
            total_ref[...],
            (((1,), (1,)), ((), ())),
            preferred_element_type=jnp.float32,
            precision=lax.Precision.HIGHEST,
        )


def norm_kernel(comb_ref, mine_ref, other_ref, gain_ref, out_ref, buf, sems):
    rows, width = comb_ref.shape
    square_sum = mine_ref[...] + other_ref[...]
    inverse = lax.rsqrt(square_sum / (HEADS * HD) + 1e-06)[:1]
    inverse = jnp.transpose(jnp.broadcast_to(inverse, (HD, rows)))
    inverse = jnp.concatenate([inverse] * (width // HD), axis=1)
    step = rows // 4
    copies = []
    for n in range(4):
        part = slice(n * step, (n + 1) * step)
        buf[part, :] = (comb_ref[part, :] * inverse[part] * gain_ref[...]).astype(jnp.bfloat16)
        copies.append(pltpu.make_async_copy(buf.at[part], out_ref.at[part], sems.at[n]))
        copies[-1].start()
    for copy in copies:
        copy.wait()


def split(keyval):
    half = pltpu.VMEM(keyval.shape[1:], keyval.dtype)
    pair = pl.pallas_call(
        split_kernel,
        in_specs=[pl.BlockSpec(memory_space=pltpu.HBM)],
        out_specs=[VMEM, VMEM],
        out_shape=[half, half],
        scratch_shapes=[pltpu.SemaphoreType.DMA((2,))],
        compiler_params=PARAMS,
        name="split",
    )(pltpu.with_memory_space_constraint(keyval, pltpu.HBM))
    return [on_chip(half) for half in pair]


def pick(come, own, *tests):
    outs = pl.pallas_call(
        functools.partial(pick_kernel, tests=tests),
        in_specs=[VMEM, VMEM],
        out_specs=[VMEM] * len(tests),
        out_shape=[pltpu.VMEM(own.shape, own.dtype)] * len(tests),
        compiler_params=PARAMS,
        name="pick",
    )(on_chip(come), own)
    return [on_chip(out) for out in outs]


def pick_both(come_k, own_k, come_v, own_v):
    outs = pl.pallas_call(
        pick_both_kernel,
        in_specs=[VMEM] * 4,
        out_specs=[VMEM] * 2,
        out_shape=[pltpu.VMEM(own_v.shape, own_v.dtype), pltpu.VMEM((2, *own_v.shape), own_v.dtype)],
        compiler_params=PARAMS,
        name="pick_both",
    )(on_chip(come_k), own_k, on_chip(come_v), own_v)
    return [on_chip(out) for out in outs]


def attend(queries, panels, ids, group, state, last):
    rows, width = queries.shape
    count = width // HD * (rows // BLK)
    if last:
        shapes = [pltpu.VMEM((rows, width), jnp.float32), pltpu.VMEM((8, rows), jnp.float32)]
    else:
        shapes = [pltpu.VMEM((count, BLK, 2 * HD), jnp.float32), pltpu.VMEM((count, BLK, HD), jnp.float32)]
    scratch = [pltpu.VMEM((rows, HD), jnp.float32)] if last else []
    first = not state
    halves = [half for i in ids for half in panels[i]]
    source = VMEM
    if first:
        shapes.append(pltpu.VMEM((rows, width), jnp.bfloat16))
        scratch.append(pltpu.SemaphoreType.DMA((width // HD // group,)))
        source = pl.BlockSpec(memory_space=pltpu.HBM)
    outs = pl.pallas_call(
        functools.partial(stage_kernel, ids=ids, group=group, first=first, last=last),
        in_specs=[source] + [VMEM] * (len(halves) + len(state)),
        out_specs=[VMEM] * len(shapes),
        out_shape=shapes,
        scratch_shapes=scratch,
        compiler_params=PARAMS,
        name="stage",
    )(queries, *halves, *state)
    return [on_chip(out) for out in outs]


UNROLL = 4
WHOLE, PREVIOUS = 4, 8
STAGES = ((0,), (5, 3), (6, 1), (4, 2, 7, 8))
ROWS, HALF_ROWS, COLS, HALF_COLS = (2, 3), (2, 2), (0, 3), (0, 2)


def local(queries, keyval, out_gain):
    tok_rows, width = queries.shape
    group = width // keyval.shape[2]
    own = split(keyval)
    r16 = [send(own[0], 1, 0, 0), send(own[1], 1, 0, 0)]
    mid = send(own[1], -1, 0, 0)
    r32 = [send(r16[0], 1, 0, 0), send(r16[1], 1, 0, 0)]
    r64 = [send(r32[0], 2, 0, 0), send(mid, -3, 0, 0)]
    (near,) = pick(r16[0], own[0], ROWS)
    r4k = send(near, 0, 1, 0)
    near, far = pick_both(r16[0], own[0], r16[1], own[1])
    r4 = [r4k, send(near, 0, 1, 0)]
    r8 = [send(far, 0, 2, 0)]
    near, far = pick(r4[0], own[0], COLS, HALF_COLS)
    r1k = send(near, 0, 0, 1)
    r2k = send(send(far, 0, 0, -1), 0, 0, -1)
    near, far = pick(r4[1], own[1], COLS, HALF_COLS)
    r1 = [r1k, send(near, 0, 0, 1)]
    r2 = [r2k, send(far, 0, 0, 2)]
    panels = [[on_chip(half) for half in panel] for panel in (own, r1, r2, r4, r8, r16, r32, r64, r1)]
    query = pltpu.with_memory_space_constraint(queries, pltpu.HBM)
    state = []
    for n, ids in enumerate(STAGES):
        state = attend(query, panels, ids, group, state, n == len(STAGES) - 1)
        if n == 0:
            *state, query = state
    comb, squares = state
    other = on_chip(lax.ppermute(squares, "head", [(0, 1), (1, 0)]))
    return pl.pallas_call(
        norm_kernel,
        in_specs=[VMEM] * 4,
        out_specs=pl.BlockSpec(memory_space=pl.ANY),
        out_shape=jax.ShapeDtypeStruct((tok_rows, width), jnp.bfloat16),
        scratch_shapes=[pltpu.VMEM((tok_rows, width), jnp.bfloat16), pltpu.SemaphoreType.DMA((4,))],
        compiler_params=PARAMS,
        name="norm",
    )(comb, squares, other, on_chip(out_gain[None, :]))


def solution(mesh):
    in_specs = (P("ctx", "head"), P(None, "ctx", "head"), P("head"))
    out_specs = P("ctx", "head")
    return jax.shard_map(local, mesh=mesh, in_specs=in_specs, out_specs=out_specs, check_vma=False)
```

```python
import functools

import jax
import jax.numpy as jnp
from jax import lax
from jax.experimental import pallas as pl
from jax.experimental.pallas import tpu as pltpu
from jax.sharding import PartitionSpec as P

HEADS = 32
HD = 128
BLK = 128
NZ, NY, NX = 8, 4, 4
NEG = -1e30
FACTOR = HD ** (-0.5) * 1.4426950408889634
VMEM = pl.BlockSpec(memory_space=pltpu.VMEM)
PARAMS = pltpu.CompilerParams(vmem_limit_bytes=16 << 20)


def on_chip(value):
    return pltpu.with_memory_space_constraint(value, pltpu.VMEM)


def ring(dz, dy, dx):
    return [
        (
            (z * NY + y) * NX + x,
            ((z + dz) % NZ * NY + (y + dy) % NY) * NX + (x + dx) % NX,
        )
        for z in range(NZ)
        for y in range(NY)
        for x in range(NX)
    ]


def send(value, dz, dy, dx):
    return lax.ppermute(value, "ctx", ring(dz, dy, dx))


def lanes(index):
    return pl.ds(index * HD if isinstance(index, int) else pl.multiple_of(index * HD, HD), HD)


def triangle():
    row = lax.broadcasted_iota(jnp.int32, (BLK, BLK), 0)
    col = lax.broadcasted_iota(jnp.int32, (BLK, BLK), 1)
    return jnp.where(row >= col, 0.0, NEG).astype(jnp.float32)


def gather_slots(panels, slots, g):
    ones = jnp.ones((BLK, HD), jnp.bfloat16)
    cut = lambda ref, j: ref[j * BLK : (j + 1) * BLK, lanes(g)]
    keys = jnp.concatenate([cut(panels[i][0], j) for i, j in slots], axis=0)
    vals = [jnp.concatenate([cut(panels[i][1], j), ones], axis=1) for i, j in slots]
    return keys, jnp.concatenate(vals, axis=0)


def score_parts(query, keys, masks):
    raw = lax.dot_general(query, keys, (((1,), (1,)), ((), ())), preferred_element_type=jnp.float32)
    parts = [raw[:, n * BLK : (n + 1) * BLK] for n in range(len(masks))]
    parts = [part if mask is None else part + mask for part, mask in zip(parts, masks)]
    top = jnp.max(functools.reduce(jnp.maximum, parts), axis=1, keepdims=True)
    return parts, top


def weigh(parts, top, vals):
    probs = [jnp.exp2((part - top) * FACTOR).astype(jnp.bfloat16) for part in parts]
    probs = jnp.concatenate(probs, axis=1)
    return lax.dot_general(probs, vals, (((1,), (0,)), ((), ())), preferred_element_type=jnp.float32)


def masks_of(slots, b):
    tri = triangle()
    place = lax.axis_index("ctx")
    masks = []
    for i, j in slots:
        if i == 0:
            masks.append(None if j == b else tri)
        else:
            masks.append(tri + jnp.where(place >= 2 ** ((i - 1) % 7), 0.0, NEG))
    return masks


def split_kernel(kv_ref, half_ref, sem, *, n):
    copy = pltpu.make_async_copy(kv_ref.at[n], half_ref, sem.at[0])
    copy.start()
    copy.wait()


def choose(moved, come_ref, own_ref, out_ref):
    @pl.when(moved)
    def _():
        out_ref[...] = come_ref[...]

    @pl.when(jnp.logical_not(moved))
    def _():
        out_ref[...] = own_ref[...]


def reaches(test):
    shift, least = test
    return ((lax.axis_index("ctx") >> shift) & 3) >= least


def pick_kernel(come_ref, own_ref, *outs, tests):
    for out_ref, test in zip(outs, tests):
        choose(reaches(test), come_ref, own_ref, out_ref)


def pick_both_kernel(come_k_ref, own_k_ref, come_v_ref, own_v_ref, near_ref, far_ref):
    choose(reaches(ROWS), come_v_ref, own_v_ref, near_ref)
    far = reaches(HALF_ROWS)
    choose(far, come_k_ref, own_k_ref, far_ref.at[0])
    choose(far, come_v_ref, own_v_ref, far_ref.at[1])


def stage_kernel(source_ref, *refs, ids, group, first, last):
    panels = {}
    q_ref = refs[-2] if first else source_ref
    for i in ids:
        if i == WHOLE:
            panels[i], refs = (refs[0].at[0], refs[0].at[1]), refs[1:]
        else:
            panels[i], refs = refs[:2], refs[2:]
    if not first:
        old_acc_ref, old_top_ref = refs[:2]
        refs = refs[2:]
    if last:
        comb_ref, sq_ref, total_ref = refs
        total_ref[...] = jnp.zeros_like(total_ref)
    else:
        acc_ref, top_ref = refs[:2]
    if first:
        width = group * HD
        loads = [
            pltpu.make_async_copy(source_ref.at[:, part], q_ref.at[:, part], refs[-1].at[n])
            for n, part in enumerate(pl.ds(n * width, width) for n in range(q_ref.shape[1] // width))
        ]
        for load in loads:
            load.start()

    def body(g, carry):
        for b in range(2):
            rows = slice(b * BLK, (b + 1) * BLK)
            slots = [(i, b) for i in ids if i != PREVIOUS]
            if b and 0 in ids:
                slots = slots + [(0, 0)]
            if not b and PREVIOUS in ids:
                slots = slots + [(PREVIOUS, 1)]
            masks = masks_of(slots, b)
            keys, vals = gather_slots(panels, slots, g)
            if last:
                total = total_ref[rows, :]
            for h in range(group):
                head = g * group + h
                unit = head * 2 + b
                parts, top = score_parts(q_ref[rows, lanes(head)], keys, masks)
                if first:
                    acc = weigh(parts, top, vals)
                else:
                    old = old_top_ref[unit]
                    top = jnp.maximum(old, top)
                    scale = jnp.exp2((old - top) * FACTOR)
                    both = weigh(parts, top, vals)
                    acc = old_acc_ref[unit] * jnp.concatenate([scale, scale], axis=1) + both
                if last:
                    comb = acc[:, :HD] / acc[:, HD:]
                    comb_ref[rows, lanes(head)] = comb
                    total = total + comb * comb
                else:
                    acc_ref[unit] = acc
                    top_ref[unit] = jnp.broadcast_to(top, (BLK, HD))
            if last:
                total_ref[rows, :] = total
        return carry

    if first:
        for g, load in enumerate(loads):
            load.wait()
            body(g, 0)
    else:
        lax.fori_loop(0, q_ref.shape[1] // HD // group, body, 0, unroll=UNROLL)
    if last:
        sq_ref[...] = lax.dot_general(
            jnp.ones((8, HD), jnp.float32),
            total_ref[...],
            (((1,), (1,)), ((), ())),
            preferred_element_type=jnp.float32,
            precision=lax.Precision.HIGHEST,
        )


def norm_kernel(comb_ref, mine_ref, other_ref, gain_ref, out_ref, buf, sems):
    rows, width = comb_ref.shape
    square_sum = mine_ref[...] + other_ref[...]
    inverse = lax.rsqrt(square_sum / (HEADS * HD) + 1e-06)[:1]
    inverse = jnp.transpose(jnp.broadcast_to(inverse, (HD, rows)))
    inverse = jnp.concatenate([inverse] * (width // HD), axis=1)
    step = rows // 4
    copies = []
    for n in range(4):
        part = slice(n * step, (n + 1) * step)
        buf[part, :] = (comb_ref[part, :] * inverse[part] * gain_ref[...]).astype(jnp.bfloat16)
        copies.append(pltpu.make_async_copy(buf.at[part], out_ref.at[part], sems.at[n]))
        copies[-1].start()
    for copy in copies:
        copy.wait()


def split(keyval, n):
    half = pl.pallas_call(
        functools.partial(split_kernel, n=n),
        in_specs=[pl.BlockSpec(memory_space=pltpu.HBM)],
        out_specs=VMEM,
        out_shape=pltpu.VMEM(keyval.shape[1:], keyval.dtype),
        scratch_shapes=[pltpu.SemaphoreType.DMA((1,))],
        compiler_params=PARAMS,
        name="split",
    )(pltpu.with_memory_space_constraint(keyval, pltpu.HBM))
    return on_chip(half)


def pick(come, own, *tests):
    outs = pl.pallas_call(
        functools.partial(pick_kernel, tests=tests),
        in_specs=[VMEM, VMEM],
        out_specs=[VMEM] * len(tests),
        out_shape=[pltpu.VMEM(own.shape, own.dtype)] * len(tests),
        compiler_params=PARAMS,
        name="pick",
    )(on_chip(come), own)
    return [on_chip(out) for out in outs]


def pick_both(come_k, own_k, come_v, own_v):
    outs = pl.pallas_call(
        pick_both_kernel,
        in_specs=[VMEM] * 4,
        out_specs=[VMEM] * 2,
        out_shape=[pltpu.VMEM(own_v.shape, own_v.dtype), pltpu.VMEM((2, *own_v.shape), own_v.dtype)],
        compiler_params=PARAMS,
        name="pick_both",
    )(on_chip(come_k), own_k, on_chip(come_v), own_v)
    return [on_chip(out) for out in outs]


def attend(queries, panels, ids, group, state, last):
    rows, width = queries.shape
    count = width // HD * (rows // BLK)
    if last:
        shapes = [pltpu.VMEM((rows, width), jnp.float32), pltpu.VMEM((8, rows), jnp.float32)]
    else:
        shapes = [pltpu.VMEM((count, BLK, 2 * HD), jnp.float32), pltpu.VMEM((count, BLK, HD), jnp.float32)]
    scratch = [pltpu.VMEM((rows, HD), jnp.float32)] if last else []
    first = not state
    halves = [half for i in ids for half in panels[i]]
    source = VMEM
    if first:
        shapes.append(pltpu.VMEM((rows, width), jnp.bfloat16))
        scratch.append(pltpu.SemaphoreType.DMA((width // HD // group,)))
        source = pl.BlockSpec(memory_space=pltpu.HBM)
    outs = pl.pallas_call(
        functools.partial(stage_kernel, ids=ids, group=group, first=first, last=last),
        in_specs=[source] + [VMEM] * (len(halves) + len(state)),
        out_specs=[VMEM] * len(shapes),
        out_shape=shapes,
        scratch_shapes=scratch,
        compiler_params=PARAMS,
        name="stage",
    )(queries, *halves, *state)
    return [on_chip(out) for out in outs]


UNROLL = 4
WHOLE, PREVIOUS = 4, 8
STAGES = ((0,), (5, 3), (6, 1, 8), (4, 2, 7))
ROWS, HALF_ROWS, COLS, HALF_COLS = (2, 3), (2, 2), (0, 3), (0, 2)


def local(queries, keyval, out_gain):
    tok_rows, width = queries.shape
    group = width // keyval.shape[2]
    own = []
    for n in range(2):
        own.append(split(keyval, n))
    r16 = [send(own[0], 1, 0, 0), send(own[1], 1, 0, 0)]
    mid = send(own[1], -1, 0, 0)
    r32 = [send(r16[0], 1, 0, 0), send(r16[1], 1, 0, 0)]
    r64 = [send(r32[0], 2, 0, 0), send(mid, -3, 0, 0)]
    (near,) = pick(r16[0], own[0], ROWS)
    r4k = send(near, 0, 1, 0)
    near, far = pick_both(r16[0], own[0], r16[1], own[1])
    r4 = [r4k, send(near, 0, 1, 0)]
    r8 = [send(far, 0, 2, 0)]
    near, far = pick(r4[0], own[0], COLS, HALF_COLS)
    r1k = send(near, 0, 0, 1)
    r2k = send(send(far, 0, 0, -1), 0, 0, -1)
    near, far = pick(r4[1], own[1], COLS, HALF_COLS)
    r1 = [r1k, send(near, 0, 0, 1)]
    r2 = [r2k, send(far, 0, 0, 2)]
    panels = [[on_chip(half) for half in panel] for panel in (own, r1, r2, r4, r8, r16, r32, r64, r1)]
    query = pltpu.with_memory_space_constraint(queries, pltpu.HBM)
    state = []
    for n, ids in enumerate(STAGES):
        state = attend(query, panels, ids, group, state, n == len(STAGES) - 1)
        if n == 0:
            *state, query = state
    comb, squares = state
    other = on_chip(lax.ppermute(squares, "head", [(0, 1), (1, 0)]))
    return pl.pallas_call(
        norm_kernel,
        in_specs=[VMEM] * 4,
        out_specs=pl.BlockSpec(memory_space=pl.ANY),
        out_shape=jax.ShapeDtypeStruct((tok_rows, width), jnp.bfloat16),
        scratch_shapes=[pltpu.VMEM((tok_rows, width), jnp.bfloat16), pltpu.SemaphoreType.DMA((4,))],
        compiler_params=PARAMS,
        name="norm",
    )(comb, squares, other, on_chip(out_gain[None, :]))


def solution(mesh):
    in_specs = (P("ctx", "head"), P(None, "ctx", "head"), P("head"))
    out_specs = P("ctx", "head")
    return jax.shard_map(local, mesh=mesh, in_specs=in_specs, out_specs=out_specs, check_vma=False)
```
